32 devices in a mesh: dp: 2 (over x), expert: 16 (over z, y, core).
Axes of the slice: x: 2, y: 2, z: 4, core: 2. Of those that a mesh axis runs over, the one named last changes fastest.
Arguments:
- tokens: bfloat16 [2048, 2048], P('expert'), may hold values from -6 to 6
- routing: int32 [2048, 8], P('expert'), may hold values from 0 to 31, all different within a row; in each aligned block of 128 rows (0 to 127, 128 to 255, ...) at most 48 rows name the same one
- route_gates: float32 [2048, 8], P('expert'), may hold values from 0.03 to 0.3
- gate_weight: bfloat16 [32, 2048, 768], P('expert', None, 'dp'), may hold values from -0.125 to 0.125
- up_weight: bfloat16 [32, 2048, 768], P('expert', None, 'dp'), may hold values from -0.125 to 0.125
- down_weight: bfloat16 [32, 2048, 768], P('expert', None, 'dp'), may hold values from -0.21875 to 0.21875
- cotangent: bfloat16 [2048, 2048], P('expert'), may hold values from -4 to 4
Outputs:
- mixed: bfloat16 [2048, 2048], P('expert', 'dp')
- token_grad: bfloat16 [2048, 2048], P('expert', 'dp')
- gates_grad: float32 [2048, 8], P('expert')
- gate_grad: bfloat16 [32, 2048, 768], P('expert', None, 'dp')
- up_grad: bfloat16 [32, 2048, 768], P('expert', None, 'dp')
- down_grad: bfloat16 [32, 2048, 768], P('expert', None, 'dp')
The draws below stay inside these ranges and needn't reach their ends.
Inputs may be any that keep to these rules, and one draw needn't show every extreme that they name: `routing`: each row names 8 different experts. Among the rows of one index of expert (aligned blocks of 128 rows) no expert is named more than 48 times, a bound that some block reaches.
All inputs are finite; a program needn't handle non-finite values.
Results may differ from the reference program's by a relative error of at most 0.012.
Values may be sent and summed in bfloat16 or wider, within the bound.
A program may use at most 192 MiB of HBM per device.

```python
import math
import jax
import jax.numpy as jnp
import numpy as np
from jax import lax

D = 2048
FF = 768
TOPK = 8
TOK_DEV = 128
EXPERTS = 32
TOKENS = 2048
CAP = 48
N_EXPERT = 16


def steps_of(rng, shape, cuts, smallest, high):
    factor_of = 1.0
    for dim, shards_of in cuts:
        steps = jax.random.uniform(jax.random.fold_in(jax.random.fold_in(rng, 6), dim), (shards_of,), jnp.float32, smallest / len(cuts), high / len(cuts))
        factor_of = factor_of * jnp.repeat(jnp.exp(steps), shape[dim] // shards_of).reshape((-1,) + (1,) * (len(shape) - 1 - dim))
    return factor_of


def deal_out(key, own, number, rows, number_of, top, most, lean):
    sequence = jax.random.permutation(key, number_of)
    crowded, common = shares(number_of, rows * top, most, lean, True), shares(number_of, rows * top, most, lean, False)
    places = jnp.arange(number_of)

    def named(tallies, rotation):
        used = int((tallies > 0).sum())
        fixed = max(1, used // 4)
        moved = fixed + (places - fixed + rotation * (used - fixed)) % max(1, number_of - fixed)
        return jnp.zeros((number_of,), jnp.int32).at[sequence[jnp.where(places < fixed, places, moved)]].set(jnp.asarray(tallies, jnp.int32))

    tallies = jnp.where(number % 4 == 0, named(crowded, number // 4), named(common, number - number // 4 - 1))
    mixed = jax.random.permutation(jax.random.fold_in(own, 3), number_of)
    source_of, taker = mixed[0:number_of // 2 * 2:2], mixed[1:number_of // 2 * 2:2]
    room = jnp.minimum(tallies[source_of] - 1, most - tallies[taker]) // 2
    room = jnp.where((source_of == sequence[0]) | (taker == sequence[0]) | (tallies[taker] == 0), 0, jnp.maximum(room, 0))
    moved = jax.random.randint(jax.random.fold_in(own, 4), (number_of // 2,), 0, 1 << 20) % (room + 1)
    tallies = tallies.at[source_of].add(-moved).at[taker].add(moved)
    members = jnp.searchsorted(jnp.cumsum(tallies), jnp.arange(rows * top), side="right").astype(jnp.int32)
    grid = members.reshape(top, rows).T
    grid = grid[jax.random.permutation(jax.random.fold_in(own, 1), rows)]
    rotation = jax.random.randint(jax.random.fold_in(own, 2), (rows, 1), 0, top)
    return jnp.take_along_axis(grid, (jnp.arange(top)[None, :] + rotation) % top, axis=1)


def shares(count, total, limit, skew, full):
    weights = [(1 << 20) // math.isqrt(grade ** skew) + 1 for grade in range(1, count + 1)]
    largest = limit if full else min(limit, max(-(-total // count), total * weights[0] // sum(weights)))
    least = 1 if total - largest >= count - 1 else 0
    holding, rest = [largest] + [least] * (count - 1), total - largest - least * (count - 1)
    while rest > 0:
        candidates = [i for i in range(1, count) if holding[i] < largest] or [i for i in range(1, count) if holding[i] < limit]
        whole, budget = sum([weights[i] for i in candidates]), rest
        for i in candidates:
            more = min(limit - holding[i], max(1, budget * weights[i] // whole), rest)
            holding[i] = holding[i] + more
            rest = rest - more
    return np.array(holding)


def centred(key, extent, scale, limit, cuts=(), kind=jnp.bfloat16):
    loudness = steps_of(key, extent, cuts, -0.22, 0.18) if cuts else 1.0
    values = jax.random.normal(key, extent, jnp.float32) * scale * loudness
    return jnp.minimum(jnp.maximum(values, -limit), limit).astype(kind)


def setup_inputs(seed: int = 0) -> dict:
    seeds = jax.random.split(jax.random.key(seed), 8)
    tokens = centred(seeds[0], (TOKENS, D), 1.0, 6.0, ((0, 16),))
    routing_keys = jax.random.split(jax.random.fold_in(seeds[1], 1), TOKENS // TOK_DEV)
    routing_turns = jax.random.permutation(jax.random.fold_in(seeds[1], 3), TOKENS // TOK_DEV)
    routing = jax.vmap(lambda own, number: deal_out(jax.random.fold_in(seeds[1], 2), own, number, TOK_DEV, EXPERTS, TOPK, CAP, 2))(routing_keys, routing_turns).reshape((TOKENS, TOPK))
    route_gates = jnp.clip(jnp.exp(math.log(0.3) - 2.3025852 * jax.random.uniform(seeds[2], (TOKENS, TOPK), jnp.float32) ** steps_of(seeds[2], (TOKENS, TOPK), ((0, 16),), -0.2, 0.2)), 0.03, 0.3)
    gate_weight = centred(seeds[3], (EXPERTS, D, FF), D ** -0.5, 0.125, ((0, 16), (2, 2)))
    up_weight = centred(seeds[4], (EXPERTS, D, FF), D ** -0.5, 0.125, ((0, 16), (2, 2)))
    down_weight = centred(seeds[5], (EXPERTS, D, FF), FF ** -0.5, 0.21875, ((0, 16), (2, 2)))
    cotangent = centred(seeds[6], (TOKENS, D), 0.5, 4.0, ((0, 16),))
    return {"tokens": tokens, "routing": routing, "route_gates": route_gates, "gate_weight": gate_weight, "up_weight": up_weight, "down_weight": down_weight, "cotangent": cotangent}


def expert_pass(slot_rows, slot_probs, slot_dout, w_gate, w_up, w_down):
    gate_pre = jnp.dot(slot_rows, w_gate, preferred_element_type=jnp.float32)
    up_pre = jnp.dot(slot_rows, w_up, preferred_element_type=jnp.float32)
    sigmoid_gate = jax.nn.sigmoid(gate_pre)
    active = gate_pre * sigmoid_gate
    hidden = (active * up_pre).astype(jnp.bfloat16)
    output = jnp.dot(hidden, w_down.T, preferred_element_type=jnp.float32).astype(jnp.bfloat16)
    slot_back = (slot_probs[:, None] * slot_dout.astype(jnp.float32)).astype(jnp.bfloat16)
    dhidden = jnp.dot(slot_back, w_down, preferred_element_type=jnp.float32)
    d_gate = (dhidden * up_pre * sigmoid_gate * (1.0 + gate_pre * (1.0 - sigmoid_gate))).astype(jnp.bfloat16)
    d_up = (dhidden * active).astype(jnp.bfloat16)
    row_grad = jnp.dot(d_gate, w_gate.T, preferred_element_type=jnp.float32)
    row_grad = (row_grad + jnp.dot(d_up, w_up.T, preferred_element_type=jnp.float32)).astype(jnp.bfloat16)
    grad_g = jnp.dot(slot_rows.T, d_gate, preferred_element_type=jnp.float32).astype(jnp.bfloat16)
    grad_u = jnp.dot(slot_rows.T, d_up, preferred_element_type=jnp.float32).astype(jnp.bfloat16)
    grad_d = jnp.dot(slot_back.T, hidden, preferred_element_type=jnp.float32).astype(jnp.bfloat16)
    return output, row_grad, grad_g, grad_u, grad_d


def reference(tokens, routing, route_gates, gate_weight, up_weight, down_weight, cotangent):
    blocks = N_EXPERT
    per_block = TOK_DEV * TOPK
    chosen = routing.reshape(blocks, per_block).astype(jnp.int32)
    one_hot = (chosen[:, :, None] == jnp.arange(EXPERTS, dtype=jnp.int32)[None, None, :]).astype(jnp.int32)
    running = jnp.cumsum(one_hot, axis=1) - one_hot
    within = jnp.sum(running * one_hot, axis=2).astype(jnp.int32)
    position = (jnp.arange(blocks, dtype=jnp.int32)[:, None] * CAP + within).astype(jnp.int32)
    assigned = jnp.arange(blocks * per_block, dtype=jnp.int32).reshape(blocks, per_block)
    table = jnp.full((EXPERTS, blocks * CAP), -1, jnp.int32).at[chosen, position].set(assigned)
    flat_gates = route_gates.reshape(-1)

    def one_expert(expert):
        ids = table[expert]
        valid = ids >= 0
        safe = jnp.maximum(ids, 0).astype(jnp.int32)
        source = (safe // TOPK).astype(jnp.int32)
        slot_rows = jnp.where(valid[:, None], tokens[source], jnp.zeros((), jnp.bfloat16))
        slot_probs = jnp.where(valid, flat_gates[safe], jnp.zeros((), jnp.float32))
        slot_dout = jnp.where(valid[:, None], cotangent[source], jnp.zeros((), jnp.bfloat16))
        return expert_pass(slot_rows, slot_probs, slot_dout,
                           gate_weight[expert], up_weight[expert], down_weight[expert])

    outputs, row_grads, gate_grad, up_grad, down_grad = lax.map(one_expert, jnp.arange(EXPERTS, dtype=jnp.int32))
    expert_rows = outputs[chosen, position].reshape(TOKENS, TOPK, D)
    grad_rows = row_grads[chosen, position].reshape(TOKENS, TOPK, D)
    expert_f = expert_rows.astype(jnp.float32)
    mixed = jnp.einsum('tk,tkd->td', route_gates, expert_f).astype(jnp.bfloat16)
    gates_grad = jnp.einsum('td,tkd->tk', cotangent.astype(jnp.float32), expert_f)
    token_grad = jnp.sum(grad_rows.astype(jnp.float32), axis=1).astype(jnp.bfloat16)
    return mixed, token_grad, gates_grad, gate_grad, up_grad, down_grad
```

```python
import jax
import jax.numpy as jnp
from jax import lax
from jax.sharding import PartitionSpec as P


def dot(a, b, dims):
    return lax.dot_general(a, b, (dims, ((), ())), preferred_element_type=jnp.float32)


def body_whole(tokens, routing, route_gates, gate_weight, up_weight, down_weight, cotangent):
    local_count = gate_weight.shape[0]
    first = lax.axis_index("expert") * local_count

    all_tokens = lax.all_gather(tokens, "expert", axis=0, tiled=True)
    picks = routing.shape[1]
    routes = jnp.concatenate([routing.astype(jnp.float32), route_gates], axis=1)
    all_routes = lax.all_gather(routes, "expert", axis=0, tiled=True)
    all_routing, all_gates = all_routes[:, :picks].astype(jnp.int32), all_routes[:, picks:]
    all_cotangent = lax.all_gather(cotangent, "expert", axis=0, tiled=True)

    named = [all_routing == first + j for j in range(local_count)]
    gate_of = [
        jnp.sum(jnp.where(named[j], all_gates, 0.0), axis=1, keepdims=True)
        for j in range(local_count)
    ]

    saved = []
    mixed_part = None
    for j in range(local_count):
        gate_pre = dot(all_tokens, gate_weight[j], ((1,), (0,)))
        up_pre = dot(all_tokens, up_weight[j], ((1,), (0,)))
        sigmoid_gate = jax.nn.sigmoid(gate_pre)
        active = gate_pre * sigmoid_gate
        hidden = active * up_pre
        weighted_hidden = (gate_of[j] * hidden).astype(jnp.bfloat16)
        saved.append((gate_pre.astype(jnp.bfloat16), up_pre.astype(jnp.bfloat16), weighted_hidden))
    hidden_cat = jnp.concatenate([s[2] for s in saved], axis=1)
    down_cat = jnp.concatenate([down_weight[j] for j in range(local_count)], axis=1)
    mixed_part = dot(hidden_cat, down_cat, ((1,), (1,))).astype(jnp.bfloat16)
    mixed_rows = lax.psum_scatter(mixed_part, "expert", scatter_dimension=0, tiled=True)

    grads = []
    gates_part = 0.0
    for j in range(local_count):
        gate_pre, up_pre, weighted_hidden = saved[j]
        gate_pre, up_pre = gate_pre.astype(jnp.float32), up_pre.astype(jnp.float32)
        raw = dot(all_cotangent, down_weight[j], ((1,), (0,)))
        sigmoid_gate = jax.nn.sigmoid(gate_pre)
        active = gate_pre * sigmoid_gate
        pair = jnp.sum(raw * (active * up_pre), axis=1, keepdims=True)
        gates_part = gates_part + jnp.where(named[j], pair, 0.0)
        dhidden = gate_of[j] * raw
        d_gate = (dhidden * up_pre * sigmoid_gate * (1.0 + gate_pre * (1.0 - sigmoid_gate))).astype(
            jnp.bfloat16
        )
        d_up = (dhidden * active).astype(jnp.bfloat16)
        grads.append((d_gate, d_up))
    d_cat = jnp.concatenate([g for pair in grads for g in pair], axis=1)
    w_cat = jnp.concatenate(
        [w for j in range(local_count) for w in (gate_weight[j], up_weight[j])], axis=1
    )
    token_part = dot(d_cat, w_cat, ((1,), (1,))).astype(jnp.bfloat16)
    token_rows = lax.psum_scatter(token_part, "expert", scatter_dimension=0, tiled=True)
    mixed = lax.psum_scatter(mixed_rows, "dp", scatter_dimension=1, tiled=True)
    token_grad = lax.psum_scatter(token_rows, "dp", scatter_dimension=1, tiled=True)
    gates_grad = lax.psum(
        lax.psum_scatter(gates_part, "expert", scatter_dimension=0, tiled=True), "dp"
    )

    grad_g = jnp.stack([dot(all_tokens, g, ((0,), (0,))).astype(jnp.bfloat16) for g, _ in grads])
    grad_u = jnp.stack([dot(all_tokens, u, ((0,), (0,))).astype(jnp.bfloat16) for _, u in grads])
    grad_d = jnp.stack(
        [dot(all_cotangent, s[2], ((0,), (0,))).astype(jnp.bfloat16) for s in saved]
    )
    return (mixed, token_grad, gates_grad, grad_g, grad_u, grad_d)


def expert_forward(slot_rows, w_gate, w_up, w_down):
    gate_pre = jnp.einsum("jrd,jdf->jrf", slot_rows, w_gate, preferred_element_type=jnp.float32)
    up_pre = jnp.einsum("jrd,jdf->jrf", slot_rows, w_up, preferred_element_type=jnp.float32)
    sigmoid_gate = jax.nn.sigmoid(gate_pre)
    active = gate_pre * sigmoid_gate
    hidden = (active * up_pre).astype(jnp.bfloat16)
    out_part = jnp.einsum("jrf,jdf->jrd", hidden, w_down, preferred_element_type=jnp.float32)
    return (out_part, (gate_pre, up_pre, sigmoid_gate, active, hidden))


def expert_backward(slot_rows, slot_back, saved, w_gate, w_up, w_down):
    gate_pre, up_pre, sigmoid_gate, active, hidden = saved
    dhidden = jnp.einsum("jrd,jdf->jrf", slot_back, w_down, preferred_element_type=jnp.float32)
    d_gate = (dhidden * up_pre * sigmoid_gate * (1.0 + gate_pre * (1.0 - sigmoid_gate))).astype(
        jnp.bfloat16
    )
    d_up = (dhidden * active).astype(jnp.bfloat16)
    row_part = jnp.einsum("jrf,jdf->jrd", d_gate, w_gate, preferred_element_type=jnp.float32)
    row_part = row_part + jnp.einsum("jrf,jdf->jrd", d_up, w_up, preferred_element_type=jnp.float32)
    grad_g = jnp.einsum("jrd,jrf->jdf", slot_rows, d_gate, preferred_element_type=jnp.float32)
    grad_u = jnp.einsum("jrd,jrf->jdf", slot_rows, d_up, preferred_element_type=jnp.float32)
    grad_d = jnp.einsum("jrd,jrf->jdf", slot_back, hidden, preferred_element_type=jnp.float32)
    return (row_part, (grad_g, grad_u, grad_d))


def body_slots(tokens, routing, route_gates, gate_weight, up_weight, down_weight, cotangent):
    rows_here, width = tokens.shape
    picks = routing.shape[1]
    local_count = gate_weight.shape[0]
    devices = lax.axis_size("expert")
    experts_all = local_count * devices
    capacity = 3 * rows_here * picks // (2 * experts_all)
    member = lax.axis_index("dp")
    chosen = routing.reshape(-1)
    one_hot = (chosen[:, None] == jnp.arange(experts_all, dtype=jnp.int32)[None, :]).astype(
        jnp.int32
    )
    running = jnp.cumsum(one_hot, axis=0) - one_hot
    within = jnp.sum(running * one_hot, axis=1)
    owners = chosen // local_count
    slots = chosen % local_count
    source_row = jnp.arange(rows_here * picks, dtype=jnp.int32) // picks
    flat_gates = route_gates.reshape(-1)
    x_rows = tokens[source_row]
    weighted = (flat_gates[:, None] * cotangent[source_row].astype(jnp.float32)).astype(
        jnp.bfloat16
    )
    half_cap = (capacity + 1) // 2
    mine = within // half_cap == member
    local_within = jnp.clip(within - member * half_cap, 0, half_cap - 1)
    target = jnp.where(mine, owners, devices)

    def scatter_share(values):
        buffer = jnp.zeros((local_count, devices, half_cap) + values.shape[1:], values.dtype)
        return buffer.at[slots, target, local_within].set(values, mode="drop")

    def gather_share(buffer):
        picked = buffer.at[slots, target, local_within].get(mode="fill", fill_value=0)
        return jnp.where(mine[:, None], picked, jnp.zeros((), picked.dtype))

    full_gate, full_up, full_down = (
        lax.all_gather(gate_weight, "dp", axis=2, tiled=True),
        lax.all_gather(up_weight, "dp", axis=2, tiled=True),
        lax.all_gather(down_weight, "dp", axis=2, tiled=True),
    )
    got_rows, got_back = (
        lax.all_to_all(scatter_share(x_rows), "expert", split_axis=1, concat_axis=1, tiled=True),
        lax.all_to_all(scatter_share(weighted), "expert", split_axis=1, concat_axis=1, tiled=True),
    )
    slot_rows = got_rows.reshape(local_count, devices * half_cap, width)
    slot_back = got_back.reshape(local_count, devices * half_cap, width)
    out_full, saved = expert_forward(slot_rows, full_gate, full_up, full_down)
    row_full, grads_full = expert_backward(
        slot_rows, slot_back, saved, full_gate, full_up, full_down
    )
    share_shape = (local_count, devices, half_cap, width)
    back_out, back_grad = (
        lax.all_to_all(
            out_full.astype(jnp.bfloat16).reshape(share_shape),
            "expert",
            split_axis=1,
            concat_axis=1,
            tiled=True,
        ),
        lax.all_to_all(
            row_full.astype(jnp.bfloat16).reshape(share_shape),
            "expert",
            split_axis=1,
            concat_axis=1,
            tiled=True,
        ),
    )
    expert_rows = gather_share(back_out).reshape(rows_here, picks, width)
    grad_rows = gather_share(back_grad).reshape(rows_here, picks, width)
    gate_part = jnp.einsum("td,tkd->tk", cotangent, expert_rows, preferred_element_type=jnp.float32)
    mixed_part = jnp.einsum("tk,tkd->td", route_gates, expert_rows.astype(jnp.float32))
    token_part = jnp.sum(grad_rows.astype(jnp.float32), axis=1)
    mixed_sum, token_sum = (
        lax.psum_scatter(
            mixed_part.astype(jnp.bfloat16), "dp", scatter_dimension=1, tiled=True
        ).astype(jnp.float32),
        lax.psum_scatter(
            token_part.astype(jnp.bfloat16), "dp", scatter_dimension=1, tiled=True
        ).astype(jnp.float32),
    )
    mixed = mixed_sum.astype(jnp.bfloat16)
    token_grad = token_sum.astype(jnp.bfloat16)
    grad_g, grad_u, grad_d = (
        lax.psum_scatter(
            grads_full[0].astype(jnp.bfloat16), "dp", scatter_dimension=2, tiled=True
        ).astype(jnp.float32),
        lax.psum_scatter(
            grads_full[1].astype(jnp.bfloat16), "dp", scatter_dimension=2, tiled=True
        ).astype(jnp.float32),
        lax.psum_scatter(
            grads_full[2].astype(jnp.bfloat16), "dp", scatter_dimension=2, tiled=True
        ).astype(jnp.float32),
    )
    grad_g = grad_g.astype(jnp.bfloat16)
    grad_u = grad_u.astype(jnp.bfloat16)
    grad_d = grad_d.astype(jnp.bfloat16)
    gates_grad = lax.psum(gate_part, "dp")
    return (mixed, token_grad, gates_grad, grad_g, grad_u, grad_d)


def body(tokens, *rest):
    held = 8 * tokens.size * tokens.dtype.itemsize * lax.axis_size("expert")
    return (body_whole if held < 1 << 27 else body_slots)(tokens, *rest)


def solution(mesh):
    in_specs = (
        P("expert", None),
        P("expert", None),
        P("expert", None),
        P("expert", None, "dp"),
        P("expert", None, "dp"),
        P("expert", None, "dp"),
        P("expert", None),
    )
    out_specs = (
        P("expert", "dp"),
        P("expert", "dp"),
        P("expert", None),
        P("expert", None, "dp"),
        P("expert", None, "dp"),
        P("expert", None, "dp"),
    )
    return jax.shard_map(body, mesh=mesh, in_specs=in_specs, out_specs=out_specs, check_vma=False)
```
